32 devices in a mesh: gz: 16 (over z, y, core), xy: 2 (over x).
Axes of the slice: x: 2, y: 2, z: 4, core: 2. Of those that a mesh axis runs over, the one named last changes fastest.
Arguments:
- fields: float32 [2, 1024, 64, 256], P(None, 'gz', 'xy'), may hold values from -64 to 64, as said below
- threshold: float32 [2], replicated, may hold values from 0.1 to 0.6
Outputs:
- detail_one: float32 [2, 512, 64, 256], P(None, 'gz', 'xy')
- detail_two: float32 [2, 256, 64, 256], P(None, 'gz', 'xy')
- detail_three: float32 [2, 128, 64, 256], P(None, 'gz', 'xy')
- detail_four: float32 [2, 64, 64, 256], P(None, 'gz', 'xy')
- detail_five: float32 [2, 32, 64, 256], P(None, 'gz', 'xy')
- coarse: float32 [2, 32, 64, 256], P(None, 'gz', 'xy')
- band_energy: float32 [2, 6], replicated
The draws below stay inside these ranges and needn't reach their ends.
Inputs may be any that keep to these rules, and one draw needn't show every extreme that they name: Finite values; the spread of the fields varies over the grid.
All inputs are finite; a program needn't handle non-finite values.
Results may differ from the reference program's by a relative error of at most 0.00002.
Values sent between devices are 32-bit elements; how exact they have to be, the bound alone decides.
A program may use at most 64 MiB of HBM per device.

```python
import jax
import jax.numpy as jnp

NY = 256
NZ = 1024
NX = 64


def draw_fields(key, part):
    depth = jnp.arange(NZ, dtype=jnp.float32) / NZ
    across = jnp.arange(NX, dtype=jnp.float32) / NX
    scale = jnp.exp(jnp.log(4.0) * depth)[:, None, None] * (1.0 + across)[None, :, None]
    noise = jax.random.normal(jax.random.fold_in(key, 13), (2, NZ, NX, NY), jnp.float32)
    values = noise * scale[None]
    return values.astype(jnp.float32)


def setup_inputs(seed: int = 0) -> dict:
    key_of = jax.random.split(jax.random.key(seed), 3)
    return {
        "fields": draw_fields(jax.random.fold_in(key_of[2], 71), 0),
        "threshold": jnp.clip(jax.random.uniform(key_of[1], (2,), jnp.float32, 0.1, 0.6), 0.1, 0.6),
    }


ALPHA = -1.586134342059924
BETA = -0.052980118572961
GAMMA = 0.882911075530934
DELTA = 0.443506852043971
KAPPA = 1.230174104914001
SQRT_TWO = 1.4142135623730951


def right_of(evens):
    return jnp.concatenate([evens[:, 1:], evens[:, -1:]], axis=1)


def left_of(odds):
    return jnp.concatenate([odds[:, :1], odds[:, :-1]], axis=1)


def one_level(values):
    half = values.shape[1] // 2
    paired = values.reshape(values.shape[0], half, 2, values.shape[2], values.shape[3])
    evens = paired[:, :, 0]
    odds = paired[:, :, 1]
    odds = odds + ALPHA * (evens + right_of(evens))
    evens = evens + BETA * (left_of(odds) + odds)
    odds = odds + GAMMA * (evens + right_of(evens))
    evens = evens + DELTA * (left_of(odds) + odds)
    return evens * (SQRT_TWO / KAPPA), odds * (KAPPA / SQRT_TWO)


def shrink(band, limit):
    return band - jnp.clip(band, -limit, limit)


def reference(fields, threshold):
    limit = threshold.reshape(2, 1, 1, 1)
    bands = []
    approx = fields
    for level in range(5):
        approx, detail = one_level(approx)
        bands.append(shrink(detail, limit))
    bands.append(shrink(approx, limit))
    energy = jnp.stack([jnp.sum(band * band, axis=(1, 2, 3)) / (band.shape[1] * band.shape[2] * band.shape[3]) for band in bands], axis=1)
    return (bands[0], bands[1], bands[2], bands[3], bands[4], bands[5], energy)
```

```python
import functools

import jax
import jax.numpy as jnp
from jax import lax
from jax.experimental import pallas as pl
from jax.experimental.pallas import tpu as pltpu
from jax.sharding import PartitionSpec as P

ALPHA = -1.586134342059924
BETA = -0.052980118572961
GAMMA = 0.882911075530934
DELTA = 0.443506852043971
KAPPA = 1.230174104914001
SQRT_TWO = 1.4142135623730951
LEVELS = 5
MESH = pl.DeviceIdType.MESH
UP, DOWN = 0, 1
SUB = 8
ROWS = 8


def kernel(
    gz_count,
    xy_count,
    threshold_ref,
    fields_ref,
    *refs,
):
    outs = refs[: LEVELS + 1]
    energy_ref = refs[LEVELS + 1]
    inputs = refs[LEVELS + 2 : 2 * LEVELS + 2]
    send_buf, recv_buf, acc, e_send_buf, e_recv_buf = refs[2 * LEVELS + 2 : 2 * LEVELS + 7]
    in_sem, edge_sem, send_sem, recv_sem, e_send_sem, e_recv_sem = refs[2 * LEVELS + 7 :]
    field_count, layers, width, _ = fields_ref.shape
    per_field = width // ROWS
    chunks = field_count * per_field
    devices = gz_count * xy_count

    gz = lax.axis_index("gz")
    xy = lax.axis_index("xy")
    me = gz * xy_count + xy
    first = gz == 0
    last = gz == gz_count - 1
    not_first = gz > 0
    not_last = gz < gz_count - 1

    def peer(step):
        target = lax.rem(me + step, devices)
        return (target // xy_count, lax.rem(target, xy_count))

    barrier = pltpu.get_barrier_semaphore()

    @pl.loop(1, devices)
    def _(step):
        pl.semaphore_signal(barrier, inc=1, device_id=peer(step), device_id_type=MESH)

    def place(c):
        return c // per_field, pl.multiple_of(lax.rem(c, per_field) * ROWS, ROWS)

    def edge_copy(side):
        part = pl.ds(0 if side == 0 else layers - 4, 4)
        return pltpu.make_async_copy(
            fields_ref.at[:, part], inputs[0].at[:, part], edge_sem.at[side]
        )

    def body_copy(c):
        f, row = place(c)
        where = (f, pl.ds(4, layers - 8), pl.ds(row, ROWS))
        return pltpu.make_async_copy(
            fields_ref.at[where], inputs[0].at[where], in_sem.at[c]
        )

    edge_copy(0).start()
    edge_copy(1).start()

    @pl.loop(0, chunks)
    def _(c):
        body_copy(c).start()

    acc[...] = jnp.zeros_like(acc)

    def send_states(level, c):
        source = inputs[level]
        count = source.shape[1]
        f, row = place(c)
        for t in range(ROWS // SUB):
            at = pl.ds(pl.multiple_of(row + t * SUB, SUB), SUB)
            to = pl.ds(t * SUB, SUB)
            s_head, d_head, s_after = (source[f, j, at] for j in range(3))
            s_prev, d_prev, s_tail, d_tail = (source[f, count - 4 + j, at] for j in range(4))
            send_buf[level, UP, c, 0, to] = d_tail + ALPHA * s_tail
            send_buf[level, UP, c, 1, to] = s_tail + BETA * (d_prev + ALPHA * (s_prev + s_tail))
            send_buf[level, DOWN, c, 0, to] = s_head
            send_buf[level, DOWN, c, 1, to] = s_head + BETA * (d_head + ALPHA * (s_head + s_after))

    def state_copy(level, c, way):
        return pltpu.make_async_remote_copy(
            src_ref=send_buf.at[level, way, c],
            dst_ref=recv_buf.at[level, way, c],
            send_sem=send_sem.at[level, way, c],
            recv_sem=recv_sem.at[level, way, c],
            device_id={"gz": gz + 1 if way == UP else gz - 1},
            device_id_type=MESH,
        )

    def start_states(level, c):
        @pl.when(not_last)
        def _():
            state_copy(level, c, UP).start()

        @pl.when(not_first)
        def _():
            state_copy(level, c, DOWN).start()

    def wait_states(level, c):
        @pl.when(not_first)
        def _():
            state_copy(level, c, UP).wait_recv()

        @pl.when(not_last)
        def _():
            state_copy(level, c, DOWN).wait_recv()

    def full_level(level, c):
        source = inputs[level]
        half = source.shape[1] // 2
        final = level == LEVELS - 1
        f, row = place(c)
        limit = threshold_ref[f]

        def shrink(band):
            return band - jnp.minimum(jnp.maximum(band, -limit), limit)

        for t in range(ROWS // SUB):
            at = pl.ds(pl.multiple_of(row + t * SUB, SUB), SUB)
            to = pl.ds(t * SUB, SUB)
            low_x = recv_buf[level, UP, c, 0, to]
            low_y = recv_buf[level, UP, c, 1, to]
            high_p = recv_buf[level, DOWN, c, 0, to]
            high_q = recv_buf[level, DOWN, c, 1, to]
            detail_sum = None
            coarse_sum = None
            s = source[f, 0, at]
            d1_before = s1_before = d2_before = None
            for i in range(half + 1):
                if i < half:
                    if i + 1 < half:
                        s_next = source[f, 2 * i + 2, at]
                    else:
                        s_next = jnp.where(last, s, high_p)
                    d1 = source[f, 2 * i + 1, at] + ALPHA * (s + s_next)
                    if i == 0:
                        d1_before = jnp.where(first, d1, low_x + ALPHA * s)
                    s1 = s + BETA * (d1_before + d1)
                else:
                    s1 = jnp.where(last, s1_before, high_q + BETA * d1_before)
                if i == 0:
                    outer = low_y + BETA * d1_before
                    d2_before = d1_before + GAMMA * (outer + s1)
                else:
                    d2 = d1_before + GAMMA * (s1_before + s1)
                    if i == 1:
                        d2_before = jnp.where(first, d2, d2_before)
                    s2 = s1_before + DELTA * (d2_before + d2)
                    band = shrink(d2 * (KAPPA / SQRT_TWO))
                    outs[level][f, i - 1, at] = band
                    square = band * band
                    detail_sum = square if detail_sum is None else detail_sum + square
                    approx = s2 * (SQRT_TWO / KAPPA)
                    if final:
                        band = shrink(approx)
                        outs[LEVELS][f, i - 1, at] = band
                        square = band * band
                        coarse_sum = square if coarse_sum is None else coarse_sum + square
                    else:
                        inputs[level + 1][f, i - 1, at] = approx
                    d2_before = d2
                if i < half:
                    d1_before, s1_before, s = d1, s1, s_next
            acc[f, level] += detail_sum
            if final:
                acc[f, LEVELS] += coarse_sum

    edge_copy(0).wait()
    edge_copy(1).wait()

    @pl.loop(0, chunks)
    def _(c):
        send_states(0, c)

    pl.semaphore_wait(barrier, devices - 1)

    @pl.loop(0, chunks)
    def _(c):
        start_states(0, c)

    for level in range(LEVELS):

        @pl.loop(0, chunks)
        def _(c):
            if level == 0:
                body_copy(c).wait()
            wait_states(level, c)
            full_level(level, c)
            if level + 1 < LEVELS:
                send_states(level + 1, c)
                start_states(level + 1, c)

    lane = lax.broadcasted_iota(jnp.int32, (1, 128), 1)
    for f in range(field_count):
        row = jnp.zeros((1, 128), jnp.float32)
        for b in range(LEVELS + 1):
            total = jnp.sum(jnp.sum(acc[f, b], axis=0, keepdims=True), axis=1, keepdims=True)
            row = jnp.where(lane == b, total, row)
        e_send_buf[pl.ds(f, 1), :] = row

    def energy_copy(step):
        return pltpu.make_async_remote_copy(
            src_ref=e_send_buf,
            dst_ref=e_recv_buf.at[me],
            send_sem=e_send_sem,
            recv_sem=e_recv_sem,
            device_id=peer(step),
            device_id_type=MESH,
        )

    @pl.loop(1, devices)
    def _(step):
        energy_copy(step).start()

    e_recv_buf[me] = e_send_buf[...]

    others = e_recv_buf.at[pl.ds(0, devices - 1)]
    pltpu.make_async_copy(others, others, e_recv_sem).wait()

    totals = jnp.sum(e_recv_buf[...], axis=0)
    cells = jnp.ones((1, 128), jnp.float32)
    for b in range(LEVELS + 1):
        shape = outs[b].shape
        cells = jnp.where(lane == b, float(shape[1] * shape[2] * shape[3] * devices), cells)
    energy_ref[...] = (totals / cells)[:, : LEVELS + 1]

    pltpu.make_async_copy(others, others, e_send_sem).wait()

    @pl.loop(0, chunks)
    def _(c):
        for level in range(LEVELS):

            @pl.when(not_last)
            def _():
                state_copy(level, c, UP).wait_send()

            @pl.when(not_first)
            def _():
                state_copy(level, c, DOWN).wait_send()


def solution(mesh):
    gz_count, xy_count = mesh.shape["gz"], mesh.shape["xy"]
    devices = gz_count * xy_count

    def local(fields, threshold):
        field_count, layers, width, depth = fields.shape
        chunks = field_count * (width // ROWS)
        f32 = jnp.float32
        halves = [layers >> (level + 1) for level in range(LEVELS)]
        band_layers = halves + halves[-1:]
        vmem = pl.BlockSpec(memory_space=pltpu.VMEM)
        return pl.pallas_call(
            functools.partial(kernel, gz_count, xy_count),
            out_shape=tuple(
                jax.ShapeDtypeStruct((field_count, n, width, depth), f32) for n in band_layers
            )
            + (jax.ShapeDtypeStruct((field_count, LEVELS + 1), f32),),
            in_specs=[
                pl.BlockSpec(memory_space=pltpu.SMEM),
                pl.BlockSpec(memory_space=pl.ANY),
            ],
            out_specs=(vmem,) * (LEVELS + 2),
            scratch_shapes=[
                pltpu.VMEM((field_count, n, width, depth), f32) for n in [layers] + halves[:-1]
            ]
            + [
                pltpu.VMEM((LEVELS, 2, chunks, 2, ROWS, depth), f32),
                pltpu.VMEM((LEVELS, 2, chunks, 2, ROWS, depth), f32),
                pltpu.VMEM((field_count, LEVELS + 1, SUB, depth), f32),
                pltpu.VMEM((field_count, 128), f32),
                pltpu.VMEM((devices, field_count, 128), f32),
                pltpu.SemaphoreType.DMA((chunks,)),
                pltpu.SemaphoreType.DMA((2,)),
                pltpu.SemaphoreType.DMA((LEVELS, 2, chunks)),
                pltpu.SemaphoreType.DMA((LEVELS, 2, chunks)),
                pltpu.SemaphoreType.DMA,
                pltpu.SemaphoreType.DMA,
            ],
            compiler_params=pltpu.CompilerParams(
                collective_id=0,
                has_side_effects=True,
                vmem_limit_bytes=32 * 1024 * 1024,
            ),
        )(threshold, fields)

    banded = P(None, "gz", "xy", None)
    return jax.shard_map(
        local,
        mesh=mesh,
        in_specs=(banded, P()),
        out_specs=(banded,) * (LEVELS + 1) + (P(),),
        check_vma=False,
    )
```

```python
import functools

import jax
import jax.numpy as jnp
from jax import lax
from jax.experimental import pallas as pl
from jax.experimental.pallas import tpu as pltpu
from jax.sharding import PartitionSpec as P

ALPHA = -1.586134342059924
BETA = -0.052980118572961
GAMMA = 0.882911075530934
DELTA = 0.443506852043971
KAPPA = 1.230174104914001
SQRT_TWO = 1.4142135623730951
LEVELS = 5
MESH = pl.DeviceIdType.MESH
UP, DOWN = 0, 1
SUB = 8
ROWS = 8


def kernel(
    gz_count,
    xy_count,
    threshold_hbm,
    fields_ref,
    *refs,
):
    outs = refs[: LEVELS + 1]
    energy_ref = refs[LEVELS + 1]
    inputs = refs[LEVELS + 2 : 2 * LEVELS + 2]
    send_buf, recv_buf, acc, e_send_buf, e_recv_buf = refs[2 * LEVELS + 2 : 2 * LEVELS + 7]
    (threshold_ref, in_sem, edge_sem, send_sem, recv_sem, e_send_sem, e_recv_sem, limit_sem) = refs[
        2 * LEVELS + 7 :
    ]
    field_count, layers, width, _ = fields_ref.shape
    per_field = width // ROWS
    chunks = field_count * per_field
    devices = gz_count * xy_count

    gz = lax.axis_index("gz")
    xy = lax.axis_index("xy")
    me = gz * xy_count + xy
    first = gz == 0
    last = gz == gz_count - 1
    not_first = gz > 0
    not_last = gz < gz_count - 1

    def wrapped(value, step, count):
        moved = value + step
        return jnp.where(moved >= count, moved - count, moved)

    def for_peers(act):
        for across in range(1, xy_count):
            act((gz, wrapped(xy, across, xy_count)))

        @pl.loop(1, gz_count)
        def _(along):
            for across in range(xy_count):
                act((wrapped(gz, along, gz_count), wrapped(xy, across, xy_count)))

    barrier = pltpu.get_barrier_semaphore()

    for_peers(
        lambda peer: pl.semaphore_signal(barrier, inc=1, device_id=peer, device_id_type=MESH)
    )

    def place(c):
        return c // per_field, pl.multiple_of(lax.rem(c, per_field) * ROWS, ROWS)

    def edge_copy(side):
        part = pl.ds(0 if side == 0 else layers - 4, 4)
        return pltpu.make_async_copy(
            fields_ref.at[:, part], inputs[0].at[:, part], edge_sem.at[side]
        )

    def body_copy(c):
        f, row = place(c)
        where = (f, pl.ds(4, layers - 8), pl.ds(row, ROWS))
        return pltpu.make_async_copy(
            fields_ref.at[where], inputs[0].at[where], in_sem.at[c]
        )

    edge_copy(0).start()
    edge_copy(1).start()
    limit_copy = pltpu.make_async_copy(threshold_hbm, threshold_ref, limit_sem)
    limit_copy.start()

    @pl.loop(0, chunks)
    def _(c):
        body_copy(c).start()

    acc[...] = jnp.zeros_like(acc)

    def send_states(level, c):
        source = inputs[level]
        count = source.shape[1]
        f, row = place(c)
        for t in range(ROWS // SUB):
            at = pl.ds(pl.multiple_of(row + t * SUB, SUB), SUB)
            to = pl.ds(t * SUB, SUB)
            s_head, d_head, s_after = (source[f, j, at] for j in range(3))
            s_prev, d_prev, s_tail, d_tail = (source[f, count - 4 + j, at] for j in range(4))
            send_buf[level, UP, c, 0, to] = d_tail + ALPHA * s_tail
            send_buf[level, UP, c, 1, to] = s_tail + BETA * (d_prev + ALPHA * (s_prev + s_tail))
            send_buf[level, DOWN, c, 0, to] = s_head
            send_buf[level, DOWN, c, 1, to] = s_head + BETA * (d_head + ALPHA * (s_head + s_after))

    def state_copy(level, c, way):
        return pltpu.make_async_remote_copy(
            src_ref=send_buf.at[level, way, c],
            dst_ref=recv_buf.at[level, way, c],
            send_sem=send_sem.at[level, way, c],
            recv_sem=recv_sem.at[level, way, c],
            device_id={"gz": gz + 1 if way == UP else gz - 1},
            device_id_type=MESH,
        )

    def start_states(level, c):
        @pl.when(not_last)
        def _():
            state_copy(level, c, UP).start()

        @pl.when(not_first)
        def _():
            state_copy(level, c, DOWN).start()

    def wait_states(level, c):
        @pl.when(not_first)
        def _():
            state_copy(level, c, UP).wait_recv()

        @pl.when(not_last)
        def _():
            state_copy(level, c, DOWN).wait_recv()

    def lift(level, c, begin, end, low, high, emit_detail, emit_approx):
        source = inputs[level]
        half = source.shape[1] // 2
        final = level == LEVELS - 1
        f, row = place(c)
        limit = threshold_ref[f]

        def shrink(band):
            return band - jnp.minimum(jnp.maximum(band, -limit), limit)

        for t in range(ROWS // SUB):
            at = pl.ds(pl.multiple_of(row + t * SUB, SUB), SUB)
            to = pl.ds(t * SUB, SUB)
            evens = lambda i: source[f, 2 * i, at]
            odds = lambda i: source[f, 2 * i + 1, at]
            d1, s1, d2, sums = {}, {}, {}, {}

            def emit(kind, ref, i, value):
                band = shrink(value)
                ref[f, i, at] = band
                square = band * band
                sums[kind] = sums[kind] + square if kind in sums else square

            s = evens(begin)
            for i in range(begin, end + 1):
                if i < end:
                    if i + 1 < half:
                        s_next = evens(i + 1)
                    else:
                        s_next = jnp.where(last, s, recv_buf[level, DOWN, c, 0, to])
                    d1[i] = odds(i) + ALPHA * (s + s_next)
                    if i == begin and low:
                        outer = recv_buf[level, UP, c, 0, to] + ALPHA * s
                        d1[i - 1] = jnp.where(first, d1[i], outer)
                    if i - 1 in d1:
                        s1[i] = s + BETA * (d1[i - 1] + d1[i])
                    if i == begin and low:
                        s1[i - 1] = recv_buf[level, UP, c, 1, to] + BETA * d1[i - 1]
                        d2[i - 1] = d1[i - 1] + GAMMA * (s1[i - 1] + s1[i])
                    s = s_next
                elif high:
                    outer = recv_buf[level, DOWN, c, 1, to] + BETA * d1[i - 1]
                    s1[i] = jnp.where(last, s1[i - 1], outer)
                if i > begin and i - 1 in s1 and i in s1:
                    d2[i - 1] = d1[i - 1] + GAMMA * (s1[i - 1] + s1[i])
                    if i - 1 == begin and low:
                        d2[i - 2] = jnp.where(first, d2[i - 1], d2[i - 2])
                    if i - 1 in emit_detail:
                        emit(level, outs[level], i - 1, d2[i - 1] * (KAPPA / SQRT_TWO))
                    if i - 1 in emit_approx:
                        s2 = s1[i - 1] + DELTA * (d2[i - 2] + d2[i - 1])
                        approx = s2 * (SQRT_TWO / KAPPA)
                        if final:
                            emit(LEVELS, outs[LEVELS], i - 1, approx)
                        else:
                            inputs[level + 1][f, i - 1, at] = approx
            for kind, total in sums.items():
                acc[f, kind] += total

    def halves_of(level):
        half = inputs[level].shape[1] // 2
        return half, half >= 8

    def interior(level, c):
        half, split = halves_of(level)
        if split:
            lift(level, c, 0, half - 1, False, False, range(1, half - 2), range(2, half - 2))

    def rim(level, c):
        half, split = halves_of(level)
        if split:
            lift(level, c, 0, 4, True, False, range(0, 1), range(0, 2))
            lift(level, c, half - 5, half, False, True, range(half - 2, half), range(half - 2, half))
        else:
            lift(level, c, 0, half, True, True, range(half), range(half))

    edge_copy(0).wait()
    edge_copy(1).wait()

    @pl.loop(0, chunks)
    def _(c):
        send_states(0, c)

    limit_copy.wait()
    pl.semaphore_wait(barrier, devices - 1)

    @pl.loop(0, chunks)
    def _(c):
        start_states(0, c)

    @pl.loop(0, chunks)
    def _(c):
        body_copy(c).wait()
        interior(0, c)

    for level in range(LEVELS):

        @pl.loop(0, chunks)
        def _(c):
            wait_states(level, c)
            rim(level, c)
            if level + 1 < LEVELS:
                send_states(level + 1, c)
                start_states(level + 1, c)
                interior(level + 1, c)

    lane = lax.broadcasted_iota(jnp.int32, (1, 128), 1)
    for f in range(field_count):
        row = jnp.zeros((1, 128), jnp.float32)
        for b in range(LEVELS + 1):
            total = jnp.sum(jnp.sum(acc[f, b], axis=0, keepdims=True), axis=1, keepdims=True)
            row = jnp.where(lane == b, total, row)
        e_send_buf[pl.ds(f, 1), :] = row

    def energy_copy(peer):
        return pltpu.make_async_remote_copy(
            src_ref=e_send_buf,
            dst_ref=e_recv_buf.at[me],
            send_sem=e_send_sem,
            recv_sem=e_recv_sem,
            device_id=peer,
            device_id_type=MESH,
        )

    for_peers(lambda peer: energy_copy(peer).start())

    e_recv_buf[me] = e_send_buf[...]

    others = e_recv_buf.at[pl.ds(0, devices - 1)]
    pltpu.make_async_copy(others, others, e_recv_sem).wait()

    totals = jnp.sum(e_recv_buf[...], axis=0)
    cells = jnp.ones((1, 128), jnp.float32)
    for b in range(LEVELS + 1):
        shape = outs[b].shape
        cells = jnp.where(lane == b, float(shape[1] * shape[2] * shape[3] * devices), cells)
    energy_ref[...] = (totals / cells)[:, : LEVELS + 1]

    pltpu.make_async_copy(others, others, e_send_sem).wait()

    @pl.loop(0, chunks)
    def _(c):
        for level in range(LEVELS):

            @pl.when(not_last)
            def _():
                state_copy(level, c, UP).wait_send()

            @pl.when(not_first)
            def _():
                state_copy(level, c, DOWN).wait_send()


def write_out(*refs):
    count = (len(refs) - 1) // 2
    sources, targets, sems = refs[:count], refs[count : 2 * count], refs[-1]
    copies = [
        pltpu.make_async_copy(source, target, sems.at[k])
        for k, (source, target) in enumerate(zip(sources, targets))
    ]
    for copy in copies:
        copy.start()
    for copy in copies:
        copy.wait()


def solution(mesh):
    gz_count, xy_count = mesh.shape["gz"], mesh.shape["xy"]
    devices = gz_count * xy_count

    def local(fields, threshold):
        field_count, layers, width, depth = fields.shape
        chunks = field_count * (width // ROWS)
        f32 = jnp.float32
        halves = [layers >> (level + 1) for level in range(LEVELS)]
        band_layers = halves + halves[-1:]
        vmem = pl.BlockSpec(memory_space=pltpu.VMEM)
        shapes = tuple(
            jax.ShapeDtypeStruct((field_count, n, width, depth), f32) for n in band_layers
        ) + (jax.ShapeDtypeStruct((field_count, LEVELS + 1), f32),)
        results = pl.pallas_call(
            functools.partial(kernel, gz_count, xy_count),
            out_shape=tuple(pltpu.VMEM(shape.shape, shape.dtype) for shape in shapes),
            in_specs=[
                pl.BlockSpec(memory_space=pltpu.HBM),
                pl.BlockSpec(memory_space=pltpu.HBM),
            ],
            out_specs=(vmem,) * (LEVELS + 2),
            scratch_shapes=[
                pltpu.VMEM((field_count, n, width, depth), f32) for n in [layers] + halves[:-1]
            ]
            + [
                pltpu.VMEM((LEVELS, 2, chunks, 2, ROWS, depth), f32),
                pltpu.VMEM((LEVELS, 2, chunks, 2, ROWS, depth), f32),
                pltpu.VMEM((field_count, LEVELS + 1, SUB, depth), f32),
                pltpu.VMEM((field_count, 128), f32),
                pltpu.VMEM((devices, field_count, 128), f32),
                pltpu.SMEM((field_count,), f32),
                pltpu.SemaphoreType.DMA((chunks,)),
                pltpu.SemaphoreType.DMA((2,)),
                pltpu.SemaphoreType.DMA((LEVELS, 2, chunks)),
                pltpu.SemaphoreType.DMA((LEVELS, 2, chunks)),
                pltpu.SemaphoreType.DMA,
                pltpu.SemaphoreType.DMA,
                pltpu.SemaphoreType.DMA,
            ],
            compiler_params=pltpu.CompilerParams(
                collective_id=0,
                has_side_effects=True,
                vmem_limit_bytes=32 * 1024 * 1024,
            ),
        )(
            pltpu.with_memory_space_constraint(threshold, pltpu.HBM),
            pltpu.with_memory_space_constraint(fields, pltpu.HBM),
        )
        return pl.pallas_call(
            write_out,
            out_shape=shapes,
            in_specs=[vmem] * (LEVELS + 2),
            out_specs=(pl.BlockSpec(memory_space=pltpu.HBM),) * (LEVELS + 2),
            scratch_shapes=[pltpu.SemaphoreType.DMA((LEVELS + 2,))],
            compiler_params=pltpu.CompilerParams(vmem_limit_bytes=4 * 1024 * 1024),
        )(*(pltpu.with_memory_space_constraint(result, pltpu.VMEM) for result in results))

    banded = P(None, "gz", "xy", None)
    return jax.shard_map(
        local,
        mesh=mesh,
        in_specs=(banded, P()),
        out_specs=(banded,) * (LEVELS + 1) + (P(),),
        check_vma=False,
    )
```

```python
import functools

import jax
import jax.numpy as jnp
from jax import lax
from jax.experimental import pallas as pl
from jax.experimental.pallas import tpu as pltpu
from jax.sharding import PartitionSpec as P

ALPHA = -1.586134342059924
BETA = -0.052980118572961
GAMMA = 0.882911075530934
DELTA = 0.443506852043971
KAPPA = 1.230174104914001
SQRT_TWO = 1.4142135623730951
LEVELS = 5
MESH = pl.DeviceIdType.MESH
UP, DOWN = 0, 1
SUB = 8
ROWS = 16


def kernel(
    gz_count,
    xy_count,
    threshold_hbm,
    fields_ref,
    *refs,
):
    outs = refs[: LEVELS + 1]
    energy_ref = refs[LEVELS + 1]
    inputs = refs[LEVELS + 2 : 2 * LEVELS + 2]
    send_buf, recv_buf, acc, e_send_buf, e_recv_buf = refs[2 * LEVELS + 2 : 2 * LEVELS + 7]
    (threshold_ref, in_sem, edge_sem, send_sem, recv_sem, e_send_sem, e_recv_sem, limit_sem) = refs[
        2 * LEVELS + 7 :
    ]
    field_count, layers, width, _ = fields_ref.shape
    per_field = width // ROWS
    chunks = field_count * per_field
    devices = gz_count * xy_count

    gz = lax.axis_index("gz")
    xy = lax.axis_index("xy")
    me = gz * xy_count + xy
    first = gz == 0
    last = gz == gz_count - 1
    not_first = gz > 0
    not_last = gz < gz_count - 1

    def wrapped(value, step, count):
        moved = value + step
        return jnp.where(moved >= count, moved - count, moved)

    def for_peers(act):
        for across in range(1, xy_count):
            act((gz, wrapped(xy, across, xy_count)))

        @pl.loop(1, gz_count)
        def _(along):
            for across in range(xy_count):
                act((wrapped(gz, along, gz_count), wrapped(xy, across, xy_count)))

    barrier = pltpu.get_barrier_semaphore()


    def place(c):
        return c // per_field, pl.multiple_of(lax.rem(c, per_field) * ROWS, ROWS)

    def edge_copy(side):
        part = pl.ds(0 if side == 0 else layers - 4, 4)
        return pltpu.make_async_copy(
            fields_ref.at[:, part], inputs[0].at[:, part], edge_sem.at[side]
        )

    def body_copy(c):
        f, row = place(c)
        where = (f, pl.ds(4, layers - 8), pl.ds(row, ROWS))
        return pltpu.make_async_copy(
            fields_ref.at[where], inputs[0].at[where], in_sem.at[c]
        )

    edge_copy(0).start()
    edge_copy(1).start()
    limit_copy = pltpu.make_async_copy(threshold_hbm, threshold_ref, limit_sem)
    limit_copy.start()
    for_peers(
        lambda peer: pl.semaphore_signal(barrier, inc=1, device_id=peer, device_id_type=MESH)
    )

    @pl.loop(0, chunks)
    def _(c):
        body_copy(c).start()

    acc[...] = jnp.zeros_like(acc)

    def send_states(level, c):
        source = inputs[level]
        count = source.shape[1]
        f, row = place(c)
        for t in range(ROWS // SUB):
            at = pl.ds(pl.multiple_of(row + t * SUB, SUB), SUB)
            to = pl.ds(t * SUB, SUB)
            s_head, d_head, s_after = (source[f, j, at] for j in range(3))
            s_prev, d_prev, s_tail, d_tail = (source[f, count - 4 + j, at] for j in range(4))
            send_buf[level, UP, c, 0, to] = d_tail + ALPHA * s_tail
            send_buf[level, UP, c, 1, to] = s_tail + BETA * (d_prev + ALPHA * (s_prev + s_tail))
            send_buf[level, DOWN, c, 0, to] = s_head
            send_buf[level, DOWN, c, 1, to] = s_head + BETA * (d_head + ALPHA * (s_head + s_after))

    def state_copy(level, c, way):
        return pltpu.make_async_remote_copy(
            src_ref=send_buf.at[level, way, c],
            dst_ref=recv_buf.at[level, way, c],
            send_sem=send_sem.at[level, way, c],
            recv_sem=recv_sem.at[level, way, c],
            device_id={"gz": gz + 1 if way == UP else gz - 1},
            device_id_type=MESH,
        )

    def start_states(level, c):
        @pl.when(not_last)
        def _():
            state_copy(level, c, UP).start()

        @pl.when(not_first)
        def _():
            state_copy(level, c, DOWN).start()

    def wait_states(level, c):
        @pl.when(not_first)
        def _():
            state_copy(level, c, UP).wait_recv()

        @pl.when(not_last)
        def _():
            state_copy(level, c, DOWN).wait_recv()

    def lift(level, c, begin, end, low, high, emit_detail, emit_approx):
        source = inputs[level]
        half = source.shape[1] // 2
        final = level == LEVELS - 1
        f, row = place(c)
        limit = threshold_ref[f]

        def shrink(band):
            return band - jnp.minimum(jnp.maximum(band, -limit), limit)

        for t in range(ROWS // SUB):
            at = pl.ds(pl.multiple_of(row + t * SUB, SUB), SUB)
            to = pl.ds(t * SUB, SUB)
            evens = lambda i: source[f, 2 * i, at]
            odds = lambda i: source[f, 2 * i + 1, at]
            d1, s1, d2, sums = {}, {}, {}, {}

            def emit(kind, ref, i, value):
                band = shrink(value)
                ref[f, i, at] = band
                square = band * band
                sums[kind] = sums[kind] + square if kind in sums else square

            s = evens(begin)
            for i in range(begin, end + 1):
                if i < end:
                    if i + 1 < half:
                        s_next = evens(i + 1)
                    else:
                        s_next = jnp.where(last, s, recv_buf[level, DOWN, c, 0, to])
                    d1[i] = odds(i) + ALPHA * (s + s_next)
                    if i == begin and low:
                        outer = recv_buf[level, UP, c, 0, to] + ALPHA * s
                        d1[i - 1] = jnp.where(first, d1[i], outer)
                    if i - 1 in d1:
                        s1[i] = s + BETA * (d1[i - 1] + d1[i])
                    if i == begin and low:
                        s1[i - 1] = recv_buf[level, UP, c, 1, to] + BETA * d1[i - 1]
                        d2[i - 1] = d1[i - 1] + GAMMA * (s1[i - 1] + s1[i])
                    s = s_next
                elif high:
                    outer = recv_buf[level, DOWN, c, 1, to] + BETA * d1[i - 1]
                    s1[i] = jnp.where(last, s1[i - 1], outer)
                if i > begin and i - 1 in s1 and i in s1:
                    d2[i - 1] = d1[i - 1] + GAMMA * (s1[i - 1] + s1[i])
                    if i - 1 == begin and low:
                        d2[i - 2] = jnp.where(first, d2[i - 1], d2[i - 2])
                    if i - 1 in emit_detail:
                        emit(level, outs[level], i - 1, d2[i - 1] * (KAPPA / SQRT_TWO))
                    if i - 1 in emit_approx:
                        s2 = s1[i - 1] + DELTA * (d2[i - 2] + d2[i - 1])
                        approx = s2 * (SQRT_TWO / KAPPA)
                        if final:
                            emit(LEVELS, outs[LEVELS], i - 1, approx)
                        else:
                            inputs[level + 1][f, i - 1, at] = approx
            for kind, total in sums.items():
                acc[f, kind] += total

    def halves_of(level):
        half = inputs[level].shape[1] // 2
        return half, half >= 8

    def interior(level, c):
        half, split = halves_of(level)
        if split:
            lift(level, c, 0, half - 1, False, False, range(1, half - 2), range(2, half - 2))

    def rim(level, c):
        half, split = halves_of(level)
        if split:
            lift(level, c, 0, 4, True, False, range(0, 1), range(0, 2))
            lift(level, c, half - 5, half, False, True, range(half - 2, half), range(half - 2, half))
        else:
            lift(level, c, 0, half, True, True, range(half), range(half))

    edge_copy(0).wait()
    edge_copy(1).wait()

    @pl.loop(0, chunks)
    def _(c):
        send_states(0, c)

    limit_copy.wait()
    pl.semaphore_wait(barrier, devices - 1)

    @pl.loop(0, chunks)
    def _(c):
        start_states(0, c)

    @pl.loop(0, chunks)
    def _(c):
        body_copy(c).wait()
        interior(0, c)

    lane = lax.broadcasted_iota(jnp.int32, (1, 128), 1)

    def reduced(f, row, kinds):
        for b in kinds:
            total = jnp.sum(jnp.sum(acc[f, b], axis=0, keepdims=True), axis=1, keepdims=True)
            row = jnp.where(lane == b, total, row)
        return row

    rows = [jnp.zeros((1, 128), jnp.float32)] * field_count
    for level in range(LEVELS):
        if level == LEVELS - 1:
            rows = [reduced(f, row, range(LEVELS - 1)) for f, row in enumerate(rows)]

        @pl.loop(0, chunks)
        def _(c):
            wait_states(level, c)
            rim(level, c)
            if level + 1 < LEVELS:
                send_states(level + 1, c)
                start_states(level + 1, c)
                interior(level + 1, c)

    for f, row in enumerate(rows):
        e_send_buf[pl.ds(f, 1), :] = reduced(f, row, range(LEVELS - 1, LEVELS + 1))

    def energy_copy(peer):
        return pltpu.make_async_remote_copy(
            src_ref=e_send_buf,
            dst_ref=e_recv_buf.at[me],
            send_sem=e_send_sem,
            recv_sem=e_recv_sem,
            device_id=peer,
            device_id_type=MESH,
        )

    for_peers(lambda peer: energy_copy(peer).start())

    e_recv_buf[me] = e_send_buf[...]

    @pl.loop(0, chunks)
    def _(c):
        for level in range(LEVELS):

            @pl.when(not_last)
            def _():
                state_copy(level, c, UP).wait_send()

            @pl.when(not_first)
            def _():
                state_copy(level, c, DOWN).wait_send()

    others = e_recv_buf.at[pl.ds(0, devices - 1)]
    pltpu.make_async_copy(others, others, e_recv_sem).wait()

    totals = jnp.sum(e_recv_buf[...], axis=0)
    cells = jnp.ones((1, 128), jnp.float32)
    for b in range(LEVELS + 1):
        shape = outs[b].shape
        cells = jnp.where(lane == b, float(shape[1] * shape[2] * shape[3] * devices), cells)
    energy_ref[...] = (totals / cells)[:, : LEVELS + 1]

    pltpu.make_async_copy(others, others, e_send_sem).wait()


def write_out(*refs):
    count = (len(refs) - 1) // 2
    sources, targets, sems = refs[:count], refs[count : 2 * count], refs[-1]
    copies = [
        pltpu.make_async_copy(source, target, sems.at[k])
        for k, (source, target) in enumerate(zip(sources, targets))
    ]
    for copy in copies:
        copy.start()
    for copy in copies:
        copy.wait()


def solution(mesh):
    gz_count, xy_count = mesh.shape["gz"], mesh.shape["xy"]
    devices = gz_count * xy_count

    def local(fields, threshold):
        field_count, layers, width, depth = fields.shape
        chunks = field_count * (width // ROWS)
        f32 = jnp.float32
        halves = [layers >> (level + 1) for level in range(LEVELS)]
        band_layers = halves + halves[-1:]
        vmem = pl.BlockSpec(memory_space=pltpu.VMEM)
        shapes = tuple(
            jax.ShapeDtypeStruct((field_count, n, width, depth), f32) for n in band_layers
        ) + (jax.ShapeDtypeStruct((field_count, LEVELS + 1), f32),)
        results = pl.pallas_call(
            functools.partial(kernel, gz_count, xy_count),
            out_shape=tuple(pltpu.VMEM(shape.shape, shape.dtype) for shape in shapes),
            in_specs=[
                pl.BlockSpec(memory_space=pltpu.HBM),
                pl.BlockSpec(memory_space=pltpu.HBM),
            ],
            out_specs=(vmem,) * (LEVELS + 2),
            scratch_shapes=[
                pltpu.VMEM((field_count, n, width, depth), f32) for n in [layers] + halves[:-1]
            ]
            + [
                pltpu.VMEM((LEVELS, 2, chunks, 2, ROWS, depth), f32),
                pltpu.VMEM((LEVELS, 2, chunks, 2, ROWS, depth), f32),
                pltpu.VMEM((field_count, LEVELS + 1, SUB, depth), f32),
                pltpu.VMEM((field_count, 128), f32),
                pltpu.VMEM((devices, field_count, 128), f32),
                pltpu.SMEM((field_count,), f32),
                pltpu.SemaphoreType.DMA((chunks,)),
                pltpu.SemaphoreType.DMA((2,)),
                pltpu.SemaphoreType.DMA((LEVELS, 2, chunks)),
                pltpu.SemaphoreType.DMA((LEVELS, 2, chunks)),
                pltpu.SemaphoreType.DMA,
                pltpu.SemaphoreType.DMA,
                pltpu.SemaphoreType.DMA,
            ],
            compiler_params=pltpu.CompilerParams(
                collective_id=0,
                has_side_effects=True,
                vmem_limit_bytes=32 * 1024 * 1024,
            ),
        )(
            pltpu.with_memory_space_constraint(threshold, pltpu.HBM),
            pltpu.with_memory_space_constraint(fields, pltpu.HBM),
        )
        return pl.pallas_call(
            write_out,
            out_shape=shapes,
            in_specs=[vmem] * (LEVELS + 2),
            out_specs=(pl.BlockSpec(memory_space=pltpu.HBM),) * (LEVELS + 2),
            scratch_shapes=[pltpu.SemaphoreType.DMA((LEVELS + 2,))],
            compiler_params=pltpu.CompilerParams(vmem_limit_bytes=4 * 1024 * 1024),
        )(*(pltpu.with_memory_space_constraint(result, pltpu.VMEM) for result in results))

    banded = P(None, "gz", "xy", None)
    return jax.shard_map(
        local,
        mesh=mesh,
        in_specs=(banded, P()),
        out_specs=(banded,) * (LEVELS + 1) + (P(),),
        check_vma=False,
    )
```
